32 devices in a mesh: groups: 2 (over x), tok: 16 (over z, y, core).
Axes of the slice: x: 2, y: 2, z: 4, core: 2. Of those that a mesh axis runs over, the one named last changes fastest.
Arguments:
- activations: bfloat16 [8, 4096, 128], P(None, ('groups', 'tok')), parts along dimension 1, may hold values from -1.796875 to 1.796875
- gradients: bfloat16 [8, 4096, 128], P(None, ('groups', 'tok')), parts along dimension 1, may hold values from -1.796875 to 1.796875
- queries: bfloat16 [64, 4096], P(None, ('groups', 'tok')), parts along dimension 1, may hold values from -0.125 to 0.125
- layer_ids: int32 [3], replicated, may hold values from 0 to 7
Outputs:
- influence: float32 [64, 4096], P(None, ('groups', 'tok')), parts along dimension 1
The draws below stay inside these ranges and needn't reach their ends.
There are 2 independent parts, one for each index of `groups`. The reference program is written for one: setup_inputs(seed, part) draws one part's arguments, and reference() takes and returns one part's arrays. A program takes and returns all parts, laid end to end along the dimension named above; an argument that names none is the same for every part. Nothing has to cross between parts.
Inputs may be any that keep to these rules, and one draw needn't show every extreme that they name: `layer_ids`: indices of stored layers; they may repeat.
All inputs are finite; a program needn't handle non-finite values.
Results may differ from the reference program's by a relative error of at most 0.0029.
Values may be sent and summed in bfloat16 or wider, within the bound.
A program may use at most 64 MiB of HBM per device.

```python
import math
import jax
import jax.numpy as jnp
from jax import lax

R = 128
Q = 64
NL = 8
LS = 3
TOKENS = 2048


def level_of(stream_key, extent, cuts, least, high):
    def one(position, parts):
        heights = jax.random.uniform(jax.random.fold_in(jax.random.fold_in(stream_key, 6), position), (parts,), jnp.float32, least / len(cuts), high / len(cuts))
        return jnp.repeat(jnp.exp(heights), extent[position] // parts).reshape((-1,) + (1,) * (len(extent) - position - 1))

    factor_of = one(*cuts[0])
    for cut in cuts[1:]:
        factor_of = factor_of * one(*cut)
    return factor_of


def gaussian(key, shape, scale, limit, cuts=(), kind=jnp.bfloat16):
    entries = scale * jax.random.normal(key, shape, jnp.float32)
    if cuts:
        entries = entries * level_of(key, shape, cuts, -0.22, 0.18)
    return jnp.clip(entries, -limit, limit).astype(kind)


def setup_inputs(seed: int = 0, part: int = 0) -> dict:
    arg_keys = jax.random.split(jax.random.key(seed), 5)
    part_keys = jax.random.split(jax.random.fold_in(arg_keys[4], part), 5)
    return {
        "activations": gaussian(part_keys[0], (NL, TOKENS, R), 0.3, 1.796875, ((1, 16),)),
        "gradients": gaussian(part_keys[1], (NL, TOKENS, R), 0.3, 1.796875, ((1, 16),)),
        "queries": gaussian(part_keys[2], (Q, TOKENS), TOKENS ** -0.5, 0.125, ((1, 16),)),
        "layer_ids": jax.random.randint(arg_keys[3], (LS,), 0, NL).astype(jnp.int32),
    }


def reference(activations, gradients, queries, layer_ids):
    chosen_inputs = jnp.take(activations, layer_ids, axis=0).astype(jnp.float32)
    chosen_grads = jnp.take(gradients, layer_ids, axis=0).astype(jnp.float32)
    tokens = chosen_inputs.shape[1]
    block_rows = math.gcd(512, tokens)

    def block_of_rows(first_row):
        input_rows = lax.dynamic_slice_in_dim(chosen_inputs, first_row, block_rows, 1)
        grad_rows = lax.dynamic_slice_in_dim(chosen_grads, first_row, block_rows, 1)
        kernel = jnp.zeros((block_rows, tokens), jnp.float32)
        for layer_index in range(LS):
            input_product_matrix = jnp.dot(input_rows[layer_index], chosen_inputs[layer_index].T, precision=lax.Precision.HIGHEST)
            grad_gram = jnp.dot(grad_rows[layer_index], chosen_grads[layer_index].T, precision=lax.Precision.HIGHEST)
            kernel = kernel + input_product_matrix * grad_gram
        second_kernel_function = kernel.astype(jnp.bfloat16)
        return lax.dot_general(queries, second_kernel_function, (((1,), (1,)), ((), ())), preferred_element_type=jnp.float32)

    starts = jnp.arange(tokens // block_rows, dtype=jnp.int32) * block_rows
    pieces = lax.map(block_of_rows, starts)
    return jnp.transpose(pieces, (1, 0, 2)).reshape(queries.shape[0], tokens)
```

```python
import functools

import jax
import jax.numpy as jnp
from jax import lax
from jax.experimental import pallas as pl
from jax.experimental.pallas import tpu as pltpu
from jax.sharding import PartitionSpec as P

MESH = pl.DeviceIdType.MESH
RETURN_TYPE = jnp.bfloat16


def passed_along(block, axis, distance):
    devices = range(lax.axis_size(axis))
    route = [((i - distance) % len(devices), i) for i in devices]
    return lax.ppermute(block, axis, route)


def token_pair_function(local_token_block, passing_block):
    input_product_matrix = jnp.einsum(
        "qun,qpn->qup", local_token_block[0], passing_block[0], preferred_element_type=jnp.float32
    )
    grad_gram = jnp.einsum(
        "qun,qpn->qup", local_token_block[1], passing_block[1], preferred_element_type=jnp.float32
    )
    return jnp.sum(input_product_matrix * grad_gram, axis=0).astype(jnp.bfloat16)


def rows_term(kernel, visitor_queries):
    return lax.dot_general(
        visitor_queries, kernel, (((1,), (1,)), ((), ())), preferred_element_type=jnp.float32
    )


def one_way_ring(activations, gradients, queries, layer_ids):
    own = jnp.stack(
        [jnp.take(activations, layer_ids, axis=0), jnp.take(gradients, layer_ids, axis=0)]
    )
    influence = rows_term(token_pair_function(own, own), queries)

    def turn(_, carried_state):
        result, block, visitor_queries = carried_state
        block = passed_along(block, "tok", 1)
        visitor_queries = passed_along(visitor_queries, "tok", 1)
        result = result + rows_term(token_pair_function(own, block), visitor_queries)
        return result, block, visitor_queries

    steps = lax.axis_size("tok") - 1
    return lax.fori_loop(0, steps, turn, (influence, own, queries))[0]


def window_kernel(
    n, snake, ids, acts, grads, queries, out, data, qs, total, back, came, send, recv, bsend, brecv
):
    chips = n // 2
    reach = chips // 4
    layers = ids.shape[0]
    pieces = layers + 1
    me = lax.axis_index("tok")
    core = lax.rem(me, 2)
    chip = lax.div(me, 2)
    if snake:
        place = jnp.where(lax.rem(chip, 2) == 0, lax.div(chip, 2), chips - 1 - lax.div(chip, 2))
    else:
        place = chip

    def device_at(step):
        to = lax.rem(place + step + chips, chips)
        if snake:
            to = jnp.where(to < chips // 2, 2 * to, 2 * (chips - 1 - to) + 1)
        return {"tok": 2 * to + core}

    other = {"tok": 2 * chip + 1 - core}

    barrier = pltpu.get_barrier_semaphore()
    for step in range(1, reach + 1):
        for sign in (1, -1):
            pl.semaphore_signal(barrier, inc=1, device_id=device_at(sign * step), device_id_type=MESH)
    pl.semaphore_signal(barrier, inc=1, device_id=other, device_id_type=MESH)

    for l in range(layers):
        data[reach, 0, l, 0] = acts[ids[l]]
        data[reach, 0, l, 1] = grads[ids[l]]
    qs[reach, 0] = queries[...]
    pl.semaphore_wait(barrier, 2 * reach + 1)

    started = []

    def part(o, m, piece):
        return data.at[reach + o, m, piece] if piece < layers else qs.at[reach + o, m]

    def copy_of(way, o, to_o, to_m, piece, device):
        return pltpu.make_async_remote_copy(
            src_ref=part(o, 0, piece),
            dst_ref=part(to_o, to_m, piece),
            send_sem=send.at[way, reach + o, piece],
            recv_sem=recv.at[reach + to_o, to_m, piece],
            device_id=device,
            device_id_type=MESH,
        )

    ahead, behind = device_at(1), device_at(-1)

    def pass_on(o, piece):
        if -reach < o <= 0:
            started.append(copy_of(0, o, o - 1, 0, piece, ahead))
            started[-1].start()
        if 0 <= o < reach:
            started.append(copy_of(1, o, o + 1, 0, piece, behind))
            started[-1].start()
        started.append(copy_of(2, o, o, 1, piece, other))
        started[-1].start()

    def arrived(o, m, piece):
        if m == 1:
            copy_of(2, o, o, 1, piece, other).wait_recv()
        elif o < 0:
            copy_of(0, o + 1, o, 0, piece, ahead).wait_recv()
        else:
            copy_of(1, o - 1, o, 0, piece, behind).wait_recv()

    def term(target, source):
        kernel = None
        for l in range(layers):
            product = None
            for kind in range(2):
                rows = data[source, :, l, kind]
                rows = rows.reshape(rows.shape[0] * rows.shape[1], rows.shape[2])
                gram = lax.dot_general(
                    rows, data[target, 0, l, kind], (((1,), (1,)), ((), ())),
                    preferred_element_type=jnp.float32,
                )
                product = gram if product is None else product * gram
            kernel = product if kernel is None else kernel + product
        kernel = kernel.astype(jnp.bfloat16)
        tokens = kernel.shape[0] // 2
        return jnp.dot(
            qs[source, 0], kernel[:tokens], preferred_element_type=jnp.float32
        ) + jnp.dot(qs[source, 1], kernel[tokens:], preferred_element_type=jnp.float32)

    for piece in range(pieces):
        pass_on(0, piece)
    for j in range(1, reach + 1):
        for piece in range(pieces):
            for o in (-j, j):
                arrived(o, 0, piece)
                pass_on(o, piece)
        if j == 1:
            for piece in range(pieces):
                arrived(0, 1, piece)
            total[...] = term(reach, reach)
        for piece in range(pieces):
            for o in (-j, j):
                arrived(o, 1, piece)
        if j < reach:
            for o in (-j, j):
                total[...] += term(reach, reach + o)

    work = [(2 * reach - 2, jnp.where(core == 0, -reach, reach), jnp.where(core == 0, 2 * reach, 0))]
    for j in range(reach - 1, 0, -1):
        work.append((2 * j - 2, -j, 2 * reach))
        work.append((2 * j - 1, j, 0))

    def back_copy(slot, step):
        return pltpu.make_async_remote_copy(
            src_ref=back.at[slot],
            dst_ref=came.at[slot],
            send_sem=bsend.at[slot],
            recv_sem=brecv.at[slot],
            device_id=device_at(step),
            device_id_type=MESH,
        )

    waiting = None
    for slot, target, source in work:
        back[slot] = term(reach + target, source).astype(back.dtype)
        if waiting is not None:
            started.append(back_copy(*waiting))
            started[-1].start()
        waiting = (slot, target)
    total[...] += term(reach, 0)
    started.append(back_copy(*waiting))
    started[-1].start()
    total[...] += term(reach, 2 * reach)
    result = total[...]
    for slot, target, _ in work:
        back_copy(slot, target).wait_recv()
        result = result + came[slot].astype(jnp.float32)
    out[...] = result
    for copy in started:
        copy.wait_send()


def windows(n, snake, activations, gradients, queries, layer_ids):
    layers = layer_ids.shape[0]
    tokens, width = activations.shape[1:]
    reach = n // 8
    slots = 2 * reach + 1
    vmem = pl.BlockSpec(memory_space=pltpu.VMEM)
    return pl.pallas_call(
        functools.partial(window_kernel, n, snake),
        out_shape=jax.ShapeDtypeStruct(queries.shape, jnp.float32),
        in_specs=[pl.BlockSpec(memory_space=pltpu.SMEM), vmem, vmem, vmem],
        out_specs=vmem,
        scratch_shapes=[
            pltpu.VMEM((slots, 2, layers, 2, tokens, width), activations.dtype),
            pltpu.VMEM((slots, 2) + queries.shape, queries.dtype),
            pltpu.VMEM(queries.shape, jnp.float32),
            pltpu.VMEM((2 * reach - 1,) + queries.shape, RETURN_TYPE),
            pltpu.VMEM((2 * reach - 1,) + queries.shape, RETURN_TYPE),
            pltpu.SemaphoreType.DMA((3, slots, layers + 1)),
            pltpu.SemaphoreType.DMA((slots, 2, layers + 1)),
            pltpu.SemaphoreType.DMA((2 * reach - 1,)),
            pltpu.SemaphoreType.DMA((2 * reach - 1,)),
        ],
        compiler_params=pltpu.CompilerParams(collective_id=0, has_side_effects=True),
    )(layer_ids, activations, gradients, queries)


def longest_step(chips):
    steps = zip(chips, chips[1:] + chips[:1])
    return max(sum(abs(a - b) for a, b in zip(p, q)) for p, q in steps)


def solution(mesh):
    n = mesh.shape["tok"]
    if n % 8 == 0:
        devices = mesh.devices[0]
        snake = False
        if hasattr(devices[0], "coords"):
            chips = [tuple(d.coords) for d in devices[::2]]
            snake = longest_step(chips[::2] + chips[::-1][::2]) < longest_step(chips)
        body = functools.partial(windows, n, snake)
    else:
        body = one_way_ring
    return jax.shard_map(
        body,
        mesh=mesh,
        in_specs=(
            P(None, ("groups", "tok"), None),
            P(None, ("groups", "tok"), None),
            P(None, ("groups", "tok")),
            P(),
        ),
        out_specs=P(None, ("groups", "tok")),
        check_vma=False,
    )
```

```python
import functools

import jax
import jax.numpy as jnp
from jax import lax
from jax.experimental import pallas as pl
from jax.experimental.pallas import tpu as pltpu
from jax.sharding import PartitionSpec as P

MESH = pl.DeviceIdType.MESH
RETURN_TYPE = jnp.bfloat16


def passed_along(block, axis, distance):
    devices = range(lax.axis_size(axis))
    route = [((i - distance) % len(devices), i) for i in devices]
    return lax.ppermute(block, axis, route)


def token_pair_function(local_token_block, passing_block):
    input_product_matrix = jnp.einsum(
        "qun,qpn->qup", local_token_block[0], passing_block[0], preferred_element_type=jnp.float32
    )
    grad_gram = jnp.einsum(
        "qun,qpn->qup", local_token_block[1], passing_block[1], preferred_element_type=jnp.float32
    )
    return jnp.sum(input_product_matrix * grad_gram, axis=0).astype(jnp.bfloat16)


def rows_term(kernel, visitor_queries):
    return lax.dot_general(
        visitor_queries, kernel, (((1,), (1,)), ((), ())), preferred_element_type=jnp.float32
    )


def one_way_ring(activations, gradients, queries, layer_ids):
    own = jnp.stack(
        [jnp.take(activations, layer_ids, axis=0), jnp.take(gradients, layer_ids, axis=0)]
    )
    influence = rows_term(token_pair_function(own, own), queries)

    def turn(_, carried_state):
        result, block, visitor_queries = carried_state
        block = passed_along(block, "tok", 1)
        visitor_queries = passed_along(visitor_queries, "tok", 1)
        result = result + rows_term(token_pair_function(own, block), visitor_queries)
        return result, block, visitor_queries

    steps = lax.axis_size("tok") - 1
    return lax.fori_loop(0, steps, turn, (influence, own, queries))[0]


def window_kernel(
    n, snake, ids, acts, grads, queries, out, stored, data, qs, total, back, came, load, send, recv, bsend, brecv
):
    chips = n // 2
    reach = chips // 4
    layers = ids.shape[0]
    pieces = layers + 1
    me = lax.axis_index("tok")
    core = lax.rem(me, 2)
    chip = lax.div(me, 2)
    if snake:
        place = jnp.where(lax.rem(chip, 2) == 0, lax.div(chip, 2), chips - 1 - lax.div(chip, 2))
    else:
        place = chip

    def device_at(step):
        to = lax.rem(place + step + chips, chips)
        if snake:
            to = jnp.where(to < chips // 2, 2 * to, 2 * (chips - 1 - to) + 1)
        return {"tok": 2 * to + core}

    other = {"tok": 2 * chip + 1 - core}

    barrier = pltpu.get_barrier_semaphore()
    for sign in (1, -1):
        pl.semaphore_signal(barrier, inc=1, device_id=device_at(sign), device_id_type=MESH)
    pl.semaphore_signal(barrier, inc=1, device_id=other, device_id_type=MESH)

    loads = [
        pltpu.make_async_copy(queries, qs.at[reach, 0], load.at[0]),
        pltpu.make_async_copy(acts, stored.at[0], load.at[1]),
        pltpu.make_async_copy(grads, stored.at[1], load.at[2]),
    ]
    for copy in loads:
        copy.start()
    for copy in loads:
        copy.wait()
    for l in range(layers):
        for kind in range(2):
            data[reach, 0, l, kind] = stored[kind, ids[l]]
    pl.semaphore_wait(barrier, 3)

    started = []

    def part(o, m, piece):
        return data.at[reach + o, m, piece] if piece < layers else qs.at[reach + o, m]

    def copy_of(way, o, to_o, to_m, piece, device):
        return pltpu.make_async_remote_copy(
            src_ref=part(o, 0, piece),
            dst_ref=part(to_o, to_m, piece),
            send_sem=send.at[way, reach + o, piece],
            recv_sem=recv.at[reach + to_o, to_m, piece],
            device_id=device,
            device_id_type=MESH,
        )

    ahead, behind = device_at(1), device_at(-1)

    def pass_on(o, piece):
        if -reach < o <= 0:
            started.append(copy_of(0, o, o - 1, 0, piece, ahead))
            started[-1].start()
        if 0 <= o < reach:
            started.append(copy_of(1, o, o + 1, 0, piece, behind))
            started[-1].start()
        started.append(copy_of(2, o, o, 1, piece, other))
        started[-1].start()

    def arrived(o, m, piece):
        if m == 1:
            copy_of(2, o, o, 1, piece, other).wait_recv()
        elif o < 0:
            copy_of(0, o + 1, o, 0, piece, ahead).wait_recv()
        else:
            copy_of(1, o - 1, o, 0, piece, behind).wait_recv()

    def term(target, source):
        kernel = None
        for l in range(layers):
            product = None
            for kind in range(2):
                rows = data[source, :, l, kind]
                rows = rows.reshape(rows.shape[0] * rows.shape[1], rows.shape[2])
                gram = lax.dot_general(
                    rows, data[target, 0, l, kind], (((1,), (1,)), ((), ())),
                    preferred_element_type=jnp.float32,
                )
                product = gram if product is None else product * gram
            kernel = product if kernel is None else kernel + product
        kernel = kernel.astype(jnp.bfloat16)
        tokens = kernel.shape[0] // 2
        return jnp.dot(
            qs[source, 0], kernel[:tokens], preferred_element_type=jnp.float32
        ) + jnp.dot(qs[source, 1], kernel[tokens:], preferred_element_type=jnp.float32)

    for piece in range(pieces):
        pass_on(0, piece)
    for j in range(1, reach + 1):
        for piece in range(pieces):
            for o in (-j, j):
                arrived(o, 0, piece)
                pass_on(o, piece)
        if j == 1:
            for piece in range(pieces):
                arrived(0, 1, piece)
            total[...] = term(reach, reach)
        for piece in range(pieces):
            for o in (-j, j):
                arrived(o, 1, piece)
        if j < reach:
            for o in (-j, j):
                total[...] += term(reach, reach + o)

    work = [(2 * reach - 2, jnp.where(core == 0, -reach, reach), jnp.where(core == 0, 2 * reach, 0))]
    for j in range(reach - 1, 0, -1):
        work.append((2 * j - 2, -j, 2 * reach))
        work.append((2 * j - 1, j, 0))

    def back_copy(slot, step):
        return pltpu.make_async_remote_copy(
            src_ref=back.at[slot],
            dst_ref=came.at[slot],
            send_sem=bsend.at[slot],
            recv_sem=brecv.at[slot],
            device_id=device_at(step),
            device_id_type=MESH,
        )

    waiting = None
    for slot, target, source in work:
        back[slot] = term(reach + target, source).astype(back.dtype)
        if waiting is not None:
            started.append(back_copy(*waiting))
            started[-1].start()
        waiting = (slot, target)
    total[...] += term(reach, 0)
    started.append(back_copy(*waiting))
    started[-1].start()
    total[...] += term(reach, 2 * reach)
    result = total[...]
    for slot, target, _ in work:
        back_copy(slot, target).wait_recv()
        result = result + came[slot].astype(jnp.float32)
    out[...] = result
    for copy in started:
        copy.wait_send()


def windows(n, snake, activations, gradients, queries, layer_ids):
    layers = layer_ids.shape[0]
    tokens, width = activations.shape[1:]
    reach = n // 8
    slots = 2 * reach + 1
    vmem = pl.BlockSpec(memory_space=pltpu.VMEM)
    return pl.pallas_call(
        functools.partial(window_kernel, n, snake),
        out_shape=jax.ShapeDtypeStruct(queries.shape, jnp.float32),
        in_specs=[pl.BlockSpec(memory_space=pltpu.SMEM)] + [pl.BlockSpec(memory_space=pl.ANY)] * 3,
        out_specs=vmem,
        scratch_shapes=[
            pltpu.VMEM((2,) + activations.shape, activations.dtype),
            pltpu.VMEM((slots, 2, layers, 2, tokens, width), activations.dtype),
            pltpu.VMEM((slots, 2) + queries.shape, queries.dtype),
            pltpu.VMEM(queries.shape, jnp.float32),
            pltpu.VMEM((2 * reach - 1,) + queries.shape, RETURN_TYPE),
            pltpu.VMEM((2 * reach - 1,) + queries.shape, RETURN_TYPE),
            pltpu.SemaphoreType.DMA((3,)),
            pltpu.SemaphoreType.DMA((3, slots, layers + 1)),
            pltpu.SemaphoreType.DMA((slots, 2, layers + 1)),
            pltpu.SemaphoreType.DMA((2 * reach - 1,)),
            pltpu.SemaphoreType.DMA((2 * reach - 1,)),
        ],
        compiler_params=pltpu.CompilerParams(collective_id=0, has_side_effects=True),
    )(layer_ids, activations, gradients, queries)


def longest_step(chips):
    steps = zip(chips, chips[1:] + chips[:1])
    return max(sum(abs(a - b) for a, b in zip(p, q)) for p, q in steps)


def solution(mesh):
    n = mesh.shape["tok"]
    if n % 8 == 0:
        devices = mesh.devices[0]
        snake = False
        if hasattr(devices[0], "coords"):
            chips = [tuple(d.coords) for d in devices[::2]]
            snake = longest_step(chips[::2] + chips[::-1][::2]) < longest_step(chips)
        body = functools.partial(windows, n, snake)
    else:
        body = one_way_ring
    return jax.shard_map(
        body,
        mesh=mesh,
        in_specs=(
            P(None, ("groups", "tok"), None),
            P(None, ("groups", "tok"), None),
            P(None, ("groups", "tok")),
            P(),
        ),
        out_specs=P(None, ("groups", "tok")),
        check_vma=False,
    )
```

```python
import functools

import jax
import jax.numpy as jnp
from jax import lax
from jax.experimental import pallas as pl
from jax.experimental.pallas import tpu as pltpu
from jax.sharding import PartitionSpec as P

MESH = pl.DeviceIdType.MESH
RETURN_TYPE = jnp.bfloat16


def passed_along(block, axis, distance):
    devices = range(lax.axis_size(axis))
    route = [((i - distance) % len(devices), i) for i in devices]
    return lax.ppermute(block, axis, route)


def token_pair_function(local_token_block, passing_block):
    input_product_matrix = jnp.einsum(
        "qun,qpn->qup", local_token_block[0], passing_block[0], preferred_element_type=jnp.float32
    )
    grad_gram = jnp.einsum(
        "qun,qpn->qup", local_token_block[1], passing_block[1], preferred_element_type=jnp.float32
    )
    return jnp.sum(input_product_matrix * grad_gram, axis=0).astype(jnp.bfloat16)


def rows_term(kernel, visitor_queries):
    return lax.dot_general(
        visitor_queries, kernel, (((1,), (1,)), ((), ())), preferred_element_type=jnp.float32
    )


def one_way_ring(activations, gradients, queries, layer_ids):
    own = jnp.stack(
        [jnp.take(activations, layer_ids, axis=0), jnp.take(gradients, layer_ids, axis=0)]
    )
    influence = rows_term(token_pair_function(own, own), queries)

    def turn(_, carried_state):
        result, block, visitor_queries = carried_state
        block = passed_along(block, "tok", 1)
        visitor_queries = passed_along(visitor_queries, "tok", 1)
        result = result + rows_term(token_pair_function(own, block), visitor_queries)
        return result, block, visitor_queries

    steps = lax.axis_size("tok") - 1
    return lax.fori_loop(0, steps, turn, (influence, own, queries))[0]


def window_kernel(
    n, snake, ids, acts, grads, queries, out, stored, data, qs, total, back, came, load, send, recv, bsend, brecv
):
    chips = n // 2
    reach = chips // 4
    layers = ids.shape[0]
    pieces = layers + 1
    me = lax.axis_index("tok")
    core = lax.rem(me, 2)
    chip = lax.div(me, 2)
    if snake:
        place = jnp.where(lax.rem(chip, 2) == 0, lax.div(chip, 2), chips - 1 - lax.div(chip, 2))
    else:
        place = chip

    def device_at(step):
        to = lax.rem(place + step + chips, chips)
        if snake:
            to = jnp.where(to < chips // 2, 2 * to, 2 * (chips - 1 - to) + 1)
        return {"tok": 2 * to + core}

    other = {"tok": 2 * chip + 1 - core}

    barrier = pltpu.get_barrier_semaphore()
    for sign in (1, -1):
        pl.semaphore_signal(barrier, inc=1, device_id=device_at(sign), device_id_type=MESH)
    pl.semaphore_signal(barrier, inc=1, device_id=other, device_id_type=MESH)

    loads = [
        pltpu.make_async_copy(queries, qs.at[reach, 0], load.at[0]),
        pltpu.make_async_copy(acts, stored.at[0], load.at[1]),
        pltpu.make_async_copy(grads, stored.at[1], load.at[2]),
    ]
    for copy in loads:
        copy.start()
    for copy in loads:
        copy.wait()
    for l in range(layers):
        for kind in range(2):
            data[reach, 0, l, kind] = stored[kind, ids[l]]
    pl.semaphore_wait(barrier, 3)

    started = []

    def part(o, m, piece):
        return data.at[reach + o, m, piece] if piece < layers else qs.at[reach + o, m]

    def copy_of(way, o, to_o, to_m, piece, device):
        return pltpu.make_async_remote_copy(
            src_ref=part(o, 0, piece),
            dst_ref=part(to_o, to_m, piece),
            send_sem=send.at[way, reach + o, piece],
            recv_sem=recv.at[reach + to_o, to_m, piece],
            device_id=device,
            device_id_type=MESH,
        )

    ahead, behind = device_at(1), device_at(-1)

    def pass_on(o, piece):
        if -reach < o <= 0:
            started.append(copy_of(0, o, o - 1, 0, piece, ahead))
            started[-1].start()
        if 0 <= o < reach:
            started.append(copy_of(1, o, o + 1, 0, piece, behind))
            started[-1].start()
        started.append(copy_of(2, o, o, 1, piece, other))
        started[-1].start()

    def arrived(o, m, piece):
        if m == 1:
            copy_of(2, o, o, 1, piece, other).wait_recv()
        elif o < 0:
            copy_of(0, o + 1, o, 0, piece, ahead).wait_recv()
        else:
            copy_of(1, o - 1, o, 0, piece, behind).wait_recv()

    def term(target, source):
        kernel = None
        for l in range(layers):
            product = None
            for kind in range(2):
                rows = data[source, :, l, kind]
                rows = rows.reshape(rows.shape[0] * rows.shape[1], rows.shape[2])
                gram = lax.dot_general(
                    rows, data[target, 0, l, kind], (((1,), (1,)), ((), ())),
                    preferred_element_type=jnp.float32,
                )
                product = gram if product is None else product * gram
            kernel = product if kernel is None else kernel + product
        kernel = kernel.astype(jnp.bfloat16)
        tokens = kernel.shape[0] // 2
        return jnp.dot(
            qs[source, 0], kernel[:tokens], preferred_element_type=jnp.float32
        ) + jnp.dot(qs[source, 1], kernel[tokens:], preferred_element_type=jnp.float32)

    for piece in range(pieces):
        pass_on(0, piece)
    for j in range(1, reach + 1):
        for piece in range(pieces):
            for o in (-j, j):
                arrived(o, 0, piece)
                pass_on(o, piece)
        if j == 1:
            for piece in range(pieces):
                arrived(0, 1, piece)
            total[...] = term(reach, reach)
        for piece in range(pieces):
            for o in (-j, j):
                arrived(o, 1, piece)
        if j < reach:
            for o in (-j, j):
                total[...] += term(reach, reach + o)

    work = [(2 * reach - 2, jnp.where(core == 0, -reach, reach), jnp.where(core == 0, 2 * reach, 0))]
    for j in range(reach - 1, 0, -1):
        work.append((2 * j - 2, -j, 2 * reach))
        work.append((2 * j - 1, j, 0))

    def back_copy(slot, step):
        return pltpu.make_async_remote_copy(
            src_ref=back.at[slot],
            dst_ref=came.at[slot],
            send_sem=bsend.at[slot],
            recv_sem=brecv.at[slot],
            device_id=device_at(step),
            device_id_type=MESH,
        )

    waiting = None
    for slot, target, source in work:
        back[slot] = term(reach + target, source).astype(back.dtype)
        if waiting is not None:
            started.append(back_copy(*waiting))
            started[-1].start()
        waiting = (slot, target)
    total[...] += term(reach, 0)
    started.append(back_copy(*waiting))
    started[-1].start()
    total[...] += term(reach, 2 * reach)
    result = total[...]
    for slot, target, _ in work:
        back_copy(slot, target).wait_recv()
        result = result + came[slot].astype(jnp.float32)
    out[...] = result
    for copy in started:
        copy.wait_send()


def windows(n, snake, activations, gradients, queries, layer_ids):
    layers = layer_ids.shape[0]
    tokens, width = activations.shape[1:]
    reach = n // 8
    slots = 2 * reach + 1
    vmem = pl.BlockSpec(memory_space=pltpu.VMEM)
    return pl.pallas_call(
        functools.partial(window_kernel, n, snake),
        out_shape=pltpu.VMEM(queries.shape, jnp.float32),
        in_specs=[pl.BlockSpec(memory_space=pltpu.SMEM)] + [pl.BlockSpec(memory_space=pl.ANY)] * 3,
        out_specs=vmem,
        scratch_shapes=[
            pltpu.VMEM((2,) + activations.shape, activations.dtype),
            pltpu.VMEM((slots, 2, layers, 2, tokens, width), activations.dtype),
            pltpu.VMEM((slots, 2) + queries.shape, queries.dtype),
            pltpu.VMEM(queries.shape, jnp.float32),
            pltpu.VMEM((2 * reach - 1,) + queries.shape, RETURN_TYPE),
            pltpu.VMEM((2 * reach - 1,) + queries.shape, RETURN_TYPE),
            pltpu.SemaphoreType.DMA((3,)),
            pltpu.SemaphoreType.DMA((3, slots, layers + 1)),
            pltpu.SemaphoreType.DMA((slots, 2, layers + 1)),
            pltpu.SemaphoreType.DMA((2 * reach - 1,)),
            pltpu.SemaphoreType.DMA((2 * reach - 1,)),
        ],
        compiler_params=pltpu.CompilerParams(collective_id=0, has_side_effects=True),
    )(layer_ids, activations, gradients, queries)


def longest_step(chips):
    steps = zip(chips, chips[1:] + chips[:1])
    return max(sum(abs(a - b) for a, b in zip(p, q)) for p, q in steps)


def solution(mesh):
    n = mesh.shape["tok"]
    if n % 8 == 0:
        devices = mesh.devices[0]
        snake = False
        if hasattr(devices[0], "coords"):
            chips = [tuple(d.coords) for d in devices[::2]]
            snake = longest_step(chips[::2] + chips[::-1][::2]) < longest_step(chips)
        body = functools.partial(windows, n, snake)
    else:
        body = one_way_ring
    return jax.shard_map(
        body,
        mesh=mesh,
        in_specs=(
            P(None, ("groups", "tok"), None),
            P(None, ("groups", "tok"), None),
            P(None, ("groups", "tok")),
            P(),
        ),
        out_specs=P(None, ("groups", "tok")),
        check_vma=False,
    )
```

```python
import functools

import jax
import jax.numpy as jnp
from jax import lax
from jax.experimental import pallas as pl
from jax.experimental.pallas import tpu as pltpu
from jax.sharding import PartitionSpec as P

MESH = pl.DeviceIdType.MESH
RETURN_TYPE = jnp.bfloat16


def passed_along(block, axis, distance):
    devices = range(lax.axis_size(axis))
    route = [((i - distance) % len(devices), i) for i in devices]
    return lax.ppermute(block, axis, route)


def token_pair_function(local_token_block, passing_block):
    input_product_matrix = jnp.einsum(
        "qun,qpn->qup", local_token_block[0], passing_block[0], preferred_element_type=jnp.float32
    )
    grad_gram = jnp.einsum(
        "qun,qpn->qup", local_token_block[1], passing_block[1], preferred_element_type=jnp.float32
    )
    return jnp.sum(input_product_matrix * grad_gram, axis=0).astype(jnp.bfloat16)


def rows_term(kernel, visitor_queries):
    return lax.dot_general(
        visitor_queries, kernel, (((1,), (1,)), ((), ())), preferred_element_type=jnp.float32
    )


def one_way_ring(activations, gradients, queries, layer_ids):
    own = jnp.stack(
        [jnp.take(activations, layer_ids, axis=0), jnp.take(gradients, layer_ids, axis=0)]
    )
    influence = rows_term(token_pair_function(own, own), queries)

    def turn(_, carried_state):
        result, block, visitor_queries = carried_state
        block = passed_along(block, "tok", 1)
        visitor_queries = passed_along(visitor_queries, "tok", 1)
        result = result + rows_term(token_pair_function(own, block), visitor_queries)
        return result, block, visitor_queries

    steps = lax.axis_size("tok") - 1
    return lax.fori_loop(0, steps, turn, (influence, own, queries))[0]


def window_kernel(
    n, snake, layer_ids, acts, grads, queries, out, ids, stored, data, qs, total, back, came, load, send, recv, bsend, brecv
):
    chips = n // 2
    reach = chips // 4
    layers = ids.shape[0]
    pieces = layers + 1
    me = lax.axis_index("tok")
    core = lax.rem(me, 2)
    chip = lax.div(me, 2)
    if snake:
        place = jnp.where(lax.rem(chip, 2) == 0, lax.div(chip, 2), chips - 1 - lax.div(chip, 2))
    else:
        place = chip

    def device_at(step):
        to = lax.rem(place + step + chips, chips)
        if snake:
            to = jnp.where(to < chips // 2, 2 * to, 2 * (chips - 1 - to) + 1)
        return {"tok": 2 * to + core}

    other = {"tok": 2 * chip + 1 - core}

    barrier = pltpu.get_barrier_semaphore()
    for sign in (1, -1):
        pl.semaphore_signal(barrier, inc=1, device_id=device_at(sign), device_id_type=MESH)
    pl.semaphore_signal(barrier, inc=1, device_id=other, device_id_type=MESH)

    loads = [
        pltpu.make_async_copy(queries, qs.at[reach, 0], load.at[0]),
        pltpu.make_async_copy(acts, stored.at[0], load.at[1]),
        pltpu.make_async_copy(grads, stored.at[1], load.at[2]),
        pltpu.make_async_copy(layer_ids, ids, load.at[3]),
    ]
    for copy in loads:
        copy.start()
    for copy in loads:
        copy.wait()
    for l in range(layers):
        for kind in range(2):
            data[reach, 0, l, kind] = stored[kind, ids[l]]
    pl.semaphore_wait(barrier, 3)

    started = []

    def part(o, m, piece):
        return data.at[reach + o, m, piece] if piece < layers else qs.at[reach + o, m]

    def copy_of(way, o, to_o, to_m, piece, device):
        return pltpu.make_async_remote_copy(
            src_ref=part(o, 0, piece),
            dst_ref=part(to_o, to_m, piece),
            send_sem=send.at[way, reach + o, piece],
            recv_sem=recv.at[reach + to_o, to_m, piece],
            device_id=device,
            device_id_type=MESH,
        )

    ahead, behind = device_at(1), device_at(-1)

    def share(o, piece):
        started.append(copy_of(2, o, o, 1, piece, other))
        started[-1].start()

    def pass_on(o, piece):
        if -reach < o <= 0:
            started.append(copy_of(0, o, o - 1, 0, piece, ahead))
            started[-1].start()
        if 0 <= o < reach:
            started.append(copy_of(1, o, o + 1, 0, piece, behind))
            started[-1].start()
        if o:
            share(o, piece)

    def arrived(o, m, piece):
        if m == 1:
            copy_of(2, o, o, 1, piece, other).wait_recv()
        elif o < 0:
            copy_of(0, o + 1, o, 0, piece, ahead).wait_recv()
        else:
            copy_of(1, o - 1, o, 0, piece, behind).wait_recv()

    def term(target, source):
        kernel = None
        for l in range(layers):
            product = None
            for kind in range(2):
                rows = data[source, :, l, kind]
                rows = rows.reshape(rows.shape[0] * rows.shape[1], rows.shape[2])
                gram = lax.dot_general(
                    rows, data[target, 0, l, kind], (((1,), (1,)), ((), ())),
                    preferred_element_type=jnp.float32,
                )
                product = gram if product is None else product * gram
            kernel = product if kernel is None else kernel + product
        kernel = kernel.astype(jnp.bfloat16)
        tokens = kernel.shape[0] // 2
        return jnp.dot(
            qs[source, 0], kernel[:tokens], preferred_element_type=jnp.float32
        ) + jnp.dot(qs[source, 1], kernel[tokens:], preferred_element_type=jnp.float32)

    for piece in range(pieces):
        pass_on(0, piece)
    for piece in range(pieces):
        share(0, piece)
    for j in range(1, reach + 1):
        for piece in range(pieces):
            for o in (-j, j):
                arrived(o, 0, piece)
                pass_on(o, piece)
        if j == 1:
            for piece in range(pieces):
                arrived(0, 1, piece)
            total[...] = term(reach, reach)
        for piece in range(pieces):
            for o in (-j, j):
                arrived(o, 1, piece)
        if j < reach:
            for o in (-j, j):
                total[...] += term(reach, reach + o)

    work = [(2 * reach - 2, jnp.where(core == 0, -reach, reach), jnp.where(core == 0, 2 * reach, 0))]
    for j in range(reach - 1, 0, -1):
        work.append((2 * j - 2, -j, 2 * reach))
        work.append((2 * j - 1, j, 0))

    def back_copy(slot, step):
        return pltpu.make_async_remote_copy(
            src_ref=back.at[slot],
            dst_ref=came.at[slot],
            send_sem=bsend.at[slot],
            recv_sem=brecv.at[slot],
            device_id=device_at(step),
            device_id_type=MESH,
        )

    waiting = None
    for slot, target, source in work:
        back[slot] = term(reach + target, source).astype(back.dtype)
        if waiting is not None:
            started.append(back_copy(*waiting))
            started[-1].start()
        waiting = (slot, target)
    total[...] += term(reach, 0)
    started.append(back_copy(*waiting))
    started[-1].start()
    total[...] += term(reach, 2 * reach)
    result = total[...]
    for slot, target, _ in work:
        back_copy(slot, target).wait_recv()
        result = result + came[slot].astype(jnp.float32)
    out[...] = result
    for copy in started:
        copy.wait_send()


def windows(n, snake, activations, gradients, queries, layer_ids):
    layers = layer_ids.shape[0]
    tokens, width = activations.shape[1:]
    reach = n // 8
    slots = 2 * reach + 1
    vmem = pl.BlockSpec(memory_space=pltpu.VMEM)
    return pl.pallas_call(
        functools.partial(window_kernel, n, snake),
        out_shape=pltpu.VMEM(queries.shape, jnp.float32),
        in_specs=[pl.BlockSpec(memory_space=pl.ANY)] * 4,
        out_specs=vmem,
        scratch_shapes=[
            pltpu.SMEM(layer_ids.shape, layer_ids.dtype),
            pltpu.VMEM((2,) + activations.shape, activations.dtype),
            pltpu.VMEM((slots, 2, layers, 2, tokens, width), activations.dtype),
            pltpu.VMEM((slots, 2) + queries.shape, queries.dtype),
            pltpu.VMEM(queries.shape, jnp.float32),
            pltpu.VMEM((2 * reach - 1,) + queries.shape, RETURN_TYPE),
            pltpu.VMEM((2 * reach - 1,) + queries.shape, RETURN_TYPE),
            pltpu.SemaphoreType.DMA((4,)),
            pltpu.SemaphoreType.DMA((3, slots, layers + 1)),
            pltpu.SemaphoreType.DMA((slots, 2, layers + 1)),
            pltpu.SemaphoreType.DMA((2 * reach - 1,)),
            pltpu.SemaphoreType.DMA((2 * reach - 1,)),
        ],
        compiler_params=pltpu.CompilerParams(collective_id=0, has_side_effects=True),
    )(layer_ids, activations, gradients, queries)


def longest_step(chips):
    steps = zip(chips, chips[1:] + chips[:1])
    return max(sum(abs(a - b) for a, b in zip(p, q)) for p, q in steps)


def solution(mesh):
    n = mesh.shape["tok"]
    if n % 8 == 0:
        devices = mesh.devices[0]
        snake = False
        if hasattr(devices[0], "coords"):
            chips = [tuple(d.coords) for d in devices[::2]]
            snake = longest_step(chips[::2] + chips[::-1][::2]) < longest_step(chips)
        body = functools.partial(windows, n, snake)
    else:
        body = one_way_ring
    return jax.shard_map(
        body,
        mesh=mesh,
        in_specs=(
            P(None, ("groups", "tok"), None),
            P(None, ("groups", "tok"), None),
            P(None, ("groups", "tok")),
            P(),
        ),
        out_specs=P(None, ("groups", "tok")),
        check_vma=False,
    )
```

```python
import functools

import jax
import jax.numpy as jnp
from jax import lax
from jax.experimental import pallas as pl
from jax.experimental.pallas import tpu as pltpu
from jax.sharding import PartitionSpec as P

MESH = pl.DeviceIdType.MESH
RETURN_TYPE = jnp.bfloat16


def passed_along(block, axis, distance):
    devices = range(lax.axis_size(axis))
    route = [((i - distance) % len(devices), i) for i in devices]
    return lax.ppermute(block, axis, route)


def token_pair_function(local_token_block, passing_block):
    input_product_matrix = jnp.einsum(
        "qun,qpn->qup", local_token_block[0], passing_block[0], preferred_element_type=jnp.float32
    )
    grad_gram = jnp.einsum(
        "qun,qpn->qup", local_token_block[1], passing_block[1], preferred_element_type=jnp.float32
    )
    return jnp.sum(input_product_matrix * grad_gram, axis=0).astype(jnp.bfloat16)


def rows_term(kernel, visitor_queries):
    return lax.dot_general(
        visitor_queries, kernel, (((1,), (1,)), ((), ())), preferred_element_type=jnp.float32
    )


def one_way_ring(activations, gradients, queries, layer_ids):
    own = jnp.stack(
        [jnp.take(activations, layer_ids, axis=0), jnp.take(gradients, layer_ids, axis=0)]
    )
    influence = rows_term(token_pair_function(own, own), queries)

    def turn(_, carried_state):
        result, block, visitor_queries = carried_state
        block = passed_along(block, "tok", 1)
        visitor_queries = passed_along(visitor_queries, "tok", 1)
        result = result + rows_term(token_pair_function(own, block), visitor_queries)
        return result, block, visitor_queries

    steps = lax.axis_size("tok") - 1
    return lax.fori_loop(0, steps, turn, (influence, own, queries))[0]


def window_kernel(
    n, snake, layer_ids, acts, grads, queries, out, ids, stored, data, qs, total, back, came, load, send, recv, bsend, brecv
):
    chips = n // 2
    reach = chips // 4
    layers = ids.shape[0]
    pieces = layers + 1
    me = lax.axis_index("tok")
    core = lax.rem(me, 2)
    chip = lax.div(me, 2)
    if snake:
        place = jnp.where(lax.rem(chip, 2) == 0, lax.div(chip, 2), chips - 1 - lax.div(chip, 2))
    else:
        place = chip

    def device_at(step):
        to = lax.rem(place + step + chips, chips)
        if snake:
            to = jnp.where(to < chips // 2, 2 * to, 2 * (chips - 1 - to) + 1)
        return {"tok": 2 * to + core}

    other = {"tok": 2 * chip + 1 - core}

    barrier = pltpu.get_barrier_semaphore()
    for sign in (1, -1):
        pl.semaphore_signal(barrier, inc=1, device_id=device_at(sign), device_id_type=MESH)
    pl.semaphore_signal(barrier, inc=1, device_id=other, device_id_type=MESH)

    loads = [
        pltpu.make_async_copy(queries, qs.at[reach, 0], load.at[0]),
        pltpu.make_async_copy(acts, stored.at[0], load.at[1]),
        pltpu.make_async_copy(grads, stored.at[1], load.at[2]),
        pltpu.make_async_copy(layer_ids, ids, load.at[3]),
    ]
    for copy in loads:
        copy.start()
    for copy in loads:
        copy.wait()
    for l in range(layers):
        for kind in range(2):
            data[reach, 0, l, kind] = stored[kind, ids[l]]
    pl.semaphore_wait(barrier, 3)

    started = []

    def part(o, m, piece):
        return data.at[reach + o, m, piece] if piece < layers else qs.at[reach + o, m]

    def copy_of(way, o, to_o, to_m, piece, device):
        return pltpu.make_async_remote_copy(
            src_ref=part(o, 0, piece),
            dst_ref=part(to_o, to_m, piece),
            send_sem=send.at[way, reach + o, piece],
            recv_sem=recv.at[reach + to_o, to_m, piece],
            device_id=device,
            device_id_type=MESH,
        )

    ahead, behind = device_at(1), device_at(-1)

    def share(o, piece):
        started.append(copy_of(2, o, o, 1, piece, other))
        started[-1].start()

    def pass_on(o, piece):
        if -reach < o <= 0:
            started.append(copy_of(0, o, o - 1, 0, piece, ahead))
            started[-1].start()
        if 0 <= o < reach:
            started.append(copy_of(1, o, o + 1, 0, piece, behind))
            started[-1].start()
        if o:
            share(o, piece)

    def arrived(o, m, piece):
        if m == 1:
            copy_of(2, o, o, 1, piece, other).wait_recv()
        elif o < 0:
            copy_of(0, o + 1, o, 0, piece, ahead).wait_recv()
        else:
            copy_of(1, o - 1, o, 0, piece, behind).wait_recv()

    def term(target, source):
        kernel = None
        for l in range(layers):
            product = None
            for kind in range(2):
                rows = data[source, :, l, kind]
                rows = rows.reshape(rows.shape[0] * rows.shape[1], rows.shape[2])
                gram = lax.dot_general(
                    data[target, 0, l, kind], rows, (((1,), (1,)), ((), ())),
                    preferred_element_type=jnp.float32,
                )
                product = gram if product is None else product * gram
            kernel = product if kernel is None else kernel + product
        visitor_queries = jnp.concatenate([qs[source, 0], qs[source, 1]], axis=1)
        return rows_term(kernel.astype(jnp.bfloat16), visitor_queries)

    for piece in range(pieces):
        pass_on(0, piece)
    for piece in range(pieces):
        share(0, piece)
    for j in range(1, reach + 1):
        for piece in range(pieces):
            for o in (-j, j):
                arrived(o, 0, piece)
                pass_on(o, piece)
        if j == 1:
            for piece in range(pieces):
                arrived(0, 1, piece)
            total[...] = term(reach, reach)
        for piece in range(pieces):
            for o in (-j, j):
                arrived(o, 1, piece)
        if j < reach:
            for o in (-j, j):
                total[...] += term(reach, reach + o)

    work = [(2 * reach - 2, jnp.where(core == 0, -reach, reach), jnp.where(core == 0, 2 * reach, 0))]
    for j in range(reach - 1, 0, -1):
        work.append((2 * j - 2, -j, 2 * reach))
        work.append((2 * j - 1, j, 0))

    def back_copy(slot, step):
        return pltpu.make_async_remote_copy(
            src_ref=back.at[slot],
            dst_ref=came.at[slot],
            send_sem=bsend.at[slot],
            recv_sem=brecv.at[slot],
            device_id=device_at(step),
            device_id_type=MESH,
        )

    waiting = None
    for slot, target, source in work:
        back[slot] = term(reach + target, source).astype(back.dtype)
        if waiting is not None:
            started.append(back_copy(*waiting))
            started[-1].start()
        waiting = (slot, target)
    total[...] += term(reach, 0)
    started.append(back_copy(*waiting))
    started[-1].start()
    total[...] += term(reach, 2 * reach)
    result = total[...]
    for slot, target, _ in work:
        back_copy(slot, target).wait_recv()
        result = result + came[slot].astype(jnp.float32)
    out[...] = result
    for copy in started:
        copy.wait_send()


def windows(n, snake, activations, gradients, queries, layer_ids):
    layers = layer_ids.shape[0]
    tokens, width = activations.shape[1:]
    reach = n // 8
    slots = 2 * reach + 1
    vmem = pl.BlockSpec(memory_space=pltpu.VMEM)
    return pl.pallas_call(
        functools.partial(window_kernel, n, snake),
        out_shape=pltpu.VMEM(queries.shape, jnp.float32),
        in_specs=[pl.BlockSpec(memory_space=pl.ANY)] * 4,
        out_specs=vmem,
        scratch_shapes=[
            pltpu.SMEM(layer_ids.shape, layer_ids.dtype),
            pltpu.VMEM((2,) + activations.shape, activations.dtype),
            pltpu.VMEM((slots, 2, layers, 2, tokens, width), activations.dtype),
            pltpu.VMEM((slots, 2) + queries.shape, queries.dtype),
            pltpu.VMEM(queries.shape, jnp.float32),
            pltpu.VMEM((2 * reach - 1,) + queries.shape, RETURN_TYPE),
            pltpu.VMEM((2 * reach - 1,) + queries.shape, RETURN_TYPE),
            pltpu.SemaphoreType.DMA((4,)),
            pltpu.SemaphoreType.DMA((3, slots, layers + 1)),
            pltpu.SemaphoreType.DMA((slots, 2, layers + 1)),
            pltpu.SemaphoreType.DMA((2 * reach - 1,)),
            pltpu.SemaphoreType.DMA((2 * reach - 1,)),
        ],
        compiler_params=pltpu.CompilerParams(collective_id=0, has_side_effects=True),
    )(layer_ids, activations, gradients, queries)


def longest_step(chips):
    steps = zip(chips, chips[1:] + chips[:1])
    return max(sum(abs(a - b) for a, b in zip(p, q)) for p, q in steps)


def solution(mesh):
    n = mesh.shape["tok"]
    if n % 8 == 0:
        devices = mesh.devices[0]
        snake = False
        if hasattr(devices[0], "coords"):
            chips = [tuple(d.coords) for d in devices[::2]]
            snake = longest_step(chips[::2] + chips[::-1][::2]) < longest_step(chips)
        body = functools.partial(windows, n, snake)
    else:
        body = one_way_ring
    return jax.shard_map(
        body,
        mesh=mesh,
        in_specs=(
            P(None, ("groups", "tok"), None),
            P(None, ("groups", "tok"), None),
            P(None, ("groups", "tok")),
            P(),
        ),
        out_specs=P(None, ("groups", "tok")),
        check_vma=False,
    )
```
